32 devices in a mesh: parts: 1, node: 4 (over y, x), local: 8 (over z, core).
Axes of the slice: x: 2, y: 2, z: 4, core: 2. Of those that a mesh axis runs over, the one named last changes fastest.
Arguments:
- tokens: bfloat16 [2048, 4096], P(('parts', 'node', 'local')), may hold values from -6 to 6
- expert_ids: int32 [2048, 8], P(('parts', 'node', 'local')), may hold values from 0 to 15, all different within a row; in each aligned block of 64 rows (0 to 63, 64 to 127, ...) at most 40 rows name the same one
- gate_weights: float32 [2048, 8], P(('parts', 'node', 'local')), may hold values from 0.02 to 0.5
- w_gate: bfloat16 [4096, 12288], P(None, ('parts', 'node', 'local')), may hold values from -0.09375 to 0.09375
- w_up: bfloat16 [4096, 12288], P(None, ('parts', 'node', 'local')), may hold values from -0.09375 to 0.09375
- w_down: bfloat16 [12288, 4096], P(('parts', 'node', 'local')), may hold values from -0.21875 to 0.21875
Outputs:
- mixed: bfloat16 [2048, 4096], P(('parts', 'node', 'local'))
The draws below stay inside these ranges and needn't reach their ends.
Inputs may be any that keep to these rules, and one draw needn't show every extreme that they name: `expert_ids`: each token names 8 different experts; among the 64 tokens of one device no expert is named more than 40 times, and in some such block one expert is named exactly 40 times.
All inputs are finite; a program needn't handle non-finite values.
Results may differ from the reference program's by a relative error of at most 0.0058.
Values may be sent and summed in bfloat16 or wider, within the bound.
A program may use at most 128 MiB of HBM per device.

```python
import math
import jax
import jax.numpy as jnp
import numpy as np
from jax import lax

D = 4096
FF = 768
TOPK = 8
TOK_DEV = 64
EXPERTS = 16
CAP = 40
TOKENS = 2048


def levels(stream_key, extent, pieces, smallest, top_value):
    level = 1.0
    for dim, blocks in pieces:
        steps = jax.random.uniform(jax.random.fold_in(jax.random.fold_in(stream_key, 6), dim), (blocks,), jnp.float32, smallest / len(pieces), top_value / len(pieces))
        level = level * jnp.repeat(jnp.exp(steps), extent[dim] // blocks).reshape((-1,) + (1,) * (len(extent) - 1 - dim))
    return level


def routed_block(stream_key, own, number, rows, number_of, top, reach, skew):
    order = jax.random.permutation(stream_key, number_of)
    packed, usual = portions_of(number_of, rows * top, reach, skew, True), portions_of(number_of, rows * top, reach, skew, False)
    places = jnp.arange(number_of)

    def named(tallies, rotation):
        used = int((tallies > 0).sum())
        fixed = max(1, used // 4)
        passed = fixed + (places - fixed + rotation * (used - fixed)) % max(1, number_of - fixed)
        return jnp.zeros((number_of,), jnp.int32).at[order[jnp.where(places < fixed, places, passed)]].set(jnp.asarray(tallies, jnp.int32))

    tallies = jnp.where(number % 4 == 0, named(packed, number // 4), named(usual, number - number // 4 - 1))
    mixed = jax.random.permutation(jax.random.fold_in(own, 3), number_of)
    donor, receiver = mixed[0:number_of // 2 * 2:2], mixed[1:number_of // 2 * 2:2]
    margin = jnp.minimum(tallies[donor] - 1, reach - tallies[receiver]) // 2
    margin = jnp.where((donor == order[0]) | (receiver == order[0]) | (tallies[receiver] == 0), 0, jnp.maximum(margin, 0))
    passed = jax.random.randint(jax.random.fold_in(own, 4), (number_of // 2,), 0, 1 << 20) % (margin + 1)
    tallies = tallies.at[donor].add(-passed).at[receiver].add(passed)
    labels = jnp.searchsorted(jnp.cumsum(tallies), jnp.arange(rows * top), side="right").astype(jnp.int32)
    grid = labels.reshape(top, rows).T
    grid = grid[jax.random.permutation(jax.random.fold_in(own, 1), rows)]
    rotation = jax.random.randint(jax.random.fold_in(own, 2), (rows, 1), 0, top)
    return jnp.take_along_axis(grid, (jnp.arange(top)[None, :] + rotation) % top, axis=1)


def portions_of(amount, total, bound, skew, full):
    loads = [(1 << 20) // math.isqrt(standing ** skew) + 1 for standing in range(1, amount + 1)]
    largest = bound if full else min(bound, max(-(-total // amount), total * loads[0] // sum(loads)))
    least = 1 if total - largest >= amount - 1 else 0
    holding, spare = [largest] + [least] * (amount - 1), total - largest - least * (amount - 1)
    while spare > 0:
        movable = [i for i in range(1, amount) if holding[i] < largest] or [i for i in range(1, amount) if holding[i] < bound]
        whole, left = sum([loads[i] for i in movable]), spare
        for i in movable:
            more = min(bound - holding[i], max(1, left * loads[i] // whole), spare)
            holding[i] = holding[i] + more
            spare = spare - more
    return np.array(holding)


def gaussian(key, shape, width, reach, split=(), held_as=jnp.bfloat16):
    loudness = levels(key, shape, split, -0.22, 0.18) if split else 1.0
    array = jax.random.normal(key, shape, jnp.float32) * width * loudness
    return jnp.minimum(jnp.maximum(array, -reach), reach).astype(held_as)


def setup_inputs(seed: int = 0, part: int = 0) -> dict:
    streams_of = jax.random.split(jax.random.key(seed), 7)
    part_keys = jax.random.split(jax.random.fold_in(streams_of[6], part), 7)
    tokens = gaussian(part_keys[0], (TOKENS, D), 1.0, 6.0, ((0, 32),))
    expert_ids_keys = jax.random.split(jax.random.fold_in(part_keys[1], 1), TOKENS // TOK_DEV)
    expert_ids_turns = jax.random.permutation(jax.random.fold_in(part_keys[1], 3), TOKENS // TOK_DEV)
    expert_ids = jax.vmap(lambda own, number: routed_block(jax.random.fold_in(part_keys[1], 2), own, number, TOK_DEV, EXPERTS, TOPK, CAP, 2))(expert_ids_keys, expert_ids_turns).reshape((TOKENS, TOPK))
    gate_weights = jnp.clip(jnp.exp(math.log(0.5) - 3.218876 * jax.random.uniform(part_keys[2], (TOKENS, TOPK), jnp.float32) ** levels(part_keys[2], (TOKENS, TOPK), ((0, 32),), -0.2, 0.2)), 0.02, 0.5)
    w_gate = gaussian(part_keys[3], (D, EXPERTS * FF), D ** -0.5, 0.09375, ((1, 32),))
    w_up = gaussian(part_keys[4], (D, EXPERTS * FF), D ** -0.5, 0.09375, ((1, 32),))
    w_down = gaussian(part_keys[5], (EXPERTS * FF, D), FF ** -0.5, 0.21875, ((0, 32),))
    return dict(tokens=tokens, expert_ids=expert_ids, gate_weights=gate_weights, w_gate=w_gate, w_up=w_up, w_down=w_down)


def reference(tokens, expert_ids, gate_weights, w_gate, w_up, w_down):
    groups = TOKENS // TOK_DEV
    pairs = TOK_DEV * TOPK
    block_ids = expert_ids.reshape(groups, pairs)
    one_hot = (block_ids[:, :, None] == jnp.arange(EXPERTS, dtype=jnp.int32)[None, None, :]).astype(jnp.int32)
    earlier = jnp.cumsum(one_hot, axis=1) - one_hot
    slot_rank = jnp.sum(earlier * one_hot, axis=2).astype(jnp.int32)
    token_index = jnp.broadcast_to(jnp.arange(TOKENS, dtype=jnp.int32).reshape(groups, TOK_DEV, 1), (groups, TOK_DEV, TOPK)).reshape(groups, pairs)
    block_index = jnp.broadcast_to(jnp.arange(groups, dtype=jnp.int32)[:, None], (groups, pairs))
    table = jnp.zeros((EXPERTS, groups, CAP), jnp.int32).at[block_ids, block_index, slot_rank].set(token_index)
    filled = jnp.zeros((EXPERTS, groups, CAP), jnp.float32).at[block_ids, block_index, slot_rank].set(1.0)

    def expert_out(expert):
        rows = tokens[table[expert].reshape(-1)]
        rows = (rows.astype(jnp.float32) * filled[expert].reshape(-1, 1)).astype(jnp.bfloat16)
        start = (expert * FF).astype(jnp.int32)
        gate_cols = lax.dynamic_slice_in_dim(w_gate, start, FF, 1)
        up_cols = lax.dynamic_slice_in_dim(w_up, start, FF, 1)
        down_rows = lax.dynamic_slice_in_dim(w_down, start, FF, 0)
        gate = jnp.dot(rows, gate_cols, preferred_element_type=jnp.float32)
        upper = jnp.dot(rows, up_cols, preferred_element_type=jnp.float32)
        hidden = (jax.nn.silu(gate) * upper).astype(jnp.bfloat16)
        return jnp.dot(hidden, down_rows, preferred_element_type=jnp.float32).astype(jnp.bfloat16)

    outputs = lax.map(expert_out, jnp.arange(EXPERTS, dtype=jnp.int32))

    def combine(block):
        chosen_ids = lax.dynamic_index_in_dim(block_ids, block, 0, keepdims=False)
        ranks = lax.dynamic_index_in_dim(slot_rank, block, 0, keepdims=False)
        chosen = outputs[chosen_ids, block * CAP + ranks].reshape(TOK_DEV, TOPK, D)
        weights = lax.dynamic_slice_in_dim(gate_weights, (block * TOK_DEV).astype(jnp.int32), TOK_DEV, 0)
        return jnp.sum(weights[:, :, None] * chosen.astype(jnp.float32), axis=1).astype(jnp.bfloat16)

    mixed = lax.map(combine, jnp.arange(groups, dtype=jnp.int32))
    return mixed.reshape(TOKENS, D)
```

```python
import functools

import jax
import jax.numpy as jnp
from jax import lax
from jax.experimental import pallas as pl
from jax.experimental.pallas import tpu as pltpu
from jax.sharding import PartitionSpec as P

MESH = pl.DeviceIdType.MESH


def partner_2(value, axis, bit):
    mask = 2**bit
    pairs = [(source, source ^ mask) for source in range(lax.axis_size(axis))]
    return lax.ppermute(value, axis, pairs)


def by_slots(tokens, expert_ids, gate_weights, w_gate, w_up, w_down):
    node_count = lax.axis_size("node")
    local_count = lax.axis_size("local")
    devices = node_count * local_count
    experts = devices // 2
    tok_rows, top_count = expert_ids.shape
    width = tokens.shape[1]
    capacity = tok_rows * top_count * 5 // (4 * experts)
    flat_ids = expert_ids.reshape(-1)
    one_hot = (flat_ids[:, None] == jnp.arange(experts, dtype=jnp.int32)[None, :]).astype(jnp.int32)
    earlier = jnp.cumsum(one_hot, axis=0) - one_hot
    slot_rank = jnp.sum(earlier * one_hot, axis=1)
    slot_index = (flat_ids * capacity + slot_rank).reshape(tok_rows, top_count)
    slot_table = jnp.any(
        slot_index[None, :, :] == jnp.arange(experts * capacity, dtype=jnp.int32)[:, None, None],
        axis=2,
    ).astype(jnp.bfloat16)
    outgoing = jnp.dot(slot_table, tokens, preferred_element_type=jnp.float32).astype(jnp.bfloat16)
    outgoing = outgoing.reshape(devices, capacity // 2, width)
    partner = partner_2((w_gate, w_up, w_down), "local", 0)
    full_gate = jnp.concatenate([w_gate, partner[0]], axis=1)
    full_up = jnp.concatenate([w_up, partner[1]], axis=1)
    full_down = jnp.concatenate([w_down, partner[2]], axis=0)
    block = lax.all_to_all(outgoing, ("node", "local"), split_axis=0, concat_axis=0, tiled=True)
    rows = block.reshape(-1, width)
    gate = jnp.dot(rows, full_gate, preferred_element_type=jnp.float32)
    upper = jnp.dot(rows, full_up, preferred_element_type=jnp.float32)
    hidden = (jax.nn.silu(gate) * upper).astype(jnp.bfloat16)
    result = jnp.dot(hidden, full_down, preferred_element_type=jnp.float32).astype(jnp.bfloat16)
    processed = result.reshape(block.shape)
    returned = lax.all_to_all(processed, ("node", "local"), split_axis=0, concat_axis=0, tiled=True)
    results = returned.reshape(experts * capacity, width)
    chosen = results[slot_index]
    mixed = jnp.sum(gate_weights[:, :, None] * chosen.astype(jnp.float32), axis=1)
    return mixed.astype(jnp.bfloat16)


LANES = 128


def layer_kernel(
    nodes, columns, width, hidden_half,
    rows_ref, gate_ref, up_ref, down_ref, out_ref,
    taken, first, second, sums, firsts, seconds, finals, acts, hidden, totals,
    load_sem, swap_send, swap_recv, col_send, col_recv, own_send, own_recv, far_send, far_recv,
    one_send, one_recv, two_send, two_recv, end_send, end_recv,
):
    part, node, local = lax.axis_index("parts"), lax.axis_index("node"), lax.axis_index("local")
    column, half = local // 2, lax.rem(local, 2)
    high, low = node // 2, lax.rem(node, 2)
    count = rows_ref.shape[0]
    split = width // 2
    wide = rows_ref.shape[1]

    def at(node_index, local_index):
        return (part, node_index, local_index)

    sides = (at(high * 2 + 1 - low, local), at((1 - high) * 2 + low, local))
    twin = at(node, column * 2 + 1 - half)

    def along(step):
        low_bit = lax.rem(column, 2)
        if step & 1:
            low_bit = 1 - low_bit
        rest, bit = column // 2, 1
        place = low_bit
        while (1 << bit) < columns:
            value = lax.rem(rest, 2)
            if step >> bit & 1:
                value = 1 - value
            place = place + value * (1 << bit)
            rest, bit = rest // 2, bit + 1
        return at(node, place * 2 + half)

    peers = [along(step) for step in range(1, columns)]
    barrier = pltpu.get_barrier_semaphore()
    for peer in (*sides, twin, *peers):
        pl.semaphore_signal(barrier, inc=1, device_id=peer, device_id_type=MESH)
    pl.semaphore_wait(barrier, 3 + len(peers))

    def send(source, target, send_sem, recv_sem, peer):
        return pltpu.make_async_remote_copy(
            src_ref=source, dst_ref=target, send_sem=send_sem, recv_sem=recv_sem,
            device_id=peer, device_id_type=MESH,
        )

    everything = []

    def start(copy):
        copy.start()
        everything.append(copy)
        return copy

    def block(step, slot):
        return taken.at[step, pl.ds(slot * count, count)]

    def columns_of(side):
        return pl.ds(0, split) if side == 0 else pl.ds(split, wide - split)

    near = (
        (gate_ref, first, 0, False), (up_ref, first, 1, False), (down_ref, second, 0, True),
    )
    loads, swaps = [], []

    def spot(target, index, by_rows, other):
        place = pl.ds((index + other) * hidden_half, hidden_half)
        return target.at[place] if by_rows else target.at[:, place]

    own = [start(send(rows_ref, block(0, side + 1), own_send.at[0, side], own_recv.at[0, side], sides[side])) for side in (0, 1)]
    spread = [start(send(rows_ref, block(step, 0), col_send.at[step], col_recv.at[step], peers[step - 1])) for step in range(1, columns)]
    for number, (source, target, index, by_rows) in enumerate(near):
        swaps.append(start(send(source, spot(target, index, by_rows, 1 if by_rows else 2), swap_send.at[number], swap_recv.at[number], twin)))
    for number, (source, target, index, by_rows) in enumerate(near):
        loads.append(pltpu.make_async_copy(source, spot(target, index, by_rows, 0), load_sem.at[number]))
    loads.append(pltpu.make_async_copy(rows_ref, block(0, 0), load_sem.at[len(near)]))
    for copy in loads:
        copy.start()

    nears, fars = [own], []

    def pass_on(step):
        moved = []
        for side in (0, 1):
            nears[step][side].wait_recv()
            piece = taken.at[step, pl.ds((side + 1) * count, count), columns_of(side)]
            target = taken.at[step, pl.ds(3 * count, count), columns_of(side)]
            moved.append(start(send(piece, target, far_send.at[step, side], far_recv.at[step, side], sides[1 - side])))
        fars.append(moved)

    def share_out(step):
        spread[step - 1].wait_recv()
        nears.append([
            start(send(block(step, 0), block(step, side + 1), own_send.at[step, side], own_recv.at[step, side], sides[side]))
            for side in (0, 1)
        ])

    def compute(step):
        for copy in fars[step]:
            copy.wait_recv()
        expert = node * columns + column
        table = taken[step, :, pl.ds(width, LANES)].astype(jnp.float32)
        lane = lax.broadcasted_iota(jnp.int32, table.shape, 1)
        chosen = (lane == expert) | (lane == expert + nodes * columns) | (lane == expert + 2 * nodes * columns)
        share = jnp.sum(jnp.where(chosen, table, 0.0), axis=1, keepdims=True)
        tile = 2 * LANES

        def into(index, carry):
            place = pl.ds(pl.multiple_of(index * tile, tile), tile)
            acts[:, place] = jnp.dot(taken[step, :, pl.ds(0, width)], first[:, place], preferred_element_type=jnp.float32)
            return carry

        lax.fori_loop(0, acts.shape[1] // tile, into, 0)
        for other in (0, 1):
            gate = acts[:, pl.ds(2 * other * hidden_half, hidden_half)]
            upper = acts[:, pl.ds((2 * other + 1) * hidden_half, hidden_half)]
            hidden[:, pl.ds(other * hidden_half, hidden_half)] = (gate / (1.0 + jnp.exp(-gate)) * upper).astype(jnp.bfloat16)
        share_wide = jnp.broadcast_to(share, (4 * count, tile))
        for side in (0, 1):
            def out_of(index, carry, side=side):
                place = pl.ds(pl.multiple_of(index * tile, tile), tile)
                source = pl.ds(pl.multiple_of(side * split + index * tile, tile), tile)
                result = jnp.dot(hidden[...], second[:, source], preferred_element_type=jnp.float32)
                result = (result * share_wide).astype(jnp.bfloat16)
                order = (0, 2, 1, 3) if side == 0 else (0, 1, 2, 3)
                for slot in range(4):
                    sums[side, step, pl.ds(order[slot] * count, count), place] = result[slot * count:(slot + 1) * count]
                return carry

            lax.fori_loop(0, split // tile, out_of, 0)

    ones, twos, ends = {}, {}, {}

    def reduce_one(step):
        ones[step] = [
            start(send(sums.at[side, step, pl.ds(2 * count, 2 * count)], firsts.at[side, step], one_send.at[step, side], one_recv.at[step, side], sides[side]))
            for side in (0, 1)
        ]

    def add(side, step, start_row, rows, source):
        def body(index, carry):
            place = pl.ds(start_row + index * 16, 16)
            other = pl.ds(index * 16, 16)
            total = sums[side, step, place].astype(jnp.float32) + source[side, step, other].astype(jnp.float32)
            sums[side, step, place] = total.astype(jnp.bfloat16)
            return carry

        lax.fori_loop(0, rows // 16, body, 0)

    def reduce_two(step):
        twos[step] = []
        for side in (0, 1):
            ones[step][side].wait_recv()
            add(side, step, 0, 2 * count, firsts)
            twos[step].append(start(send(sums.at[side, step, pl.ds(count, count)], seconds.at[side, step], two_send.at[step, side], two_recv.at[step, side], sides[1 - side])))

    def reduce_end(step):
        for side in (0, 1):
            twos[step][side].wait_recv()
            add(side, step, 0, count, seconds)
        if step:
            ends[step] = [
                start(send(sums.at[side, step, pl.ds(0, count)], finals.at[side, step - 1], end_send.at[step, side], end_recv.at[step, side], peers[step - 1]))
                for side in (0, 1)
            ]

    pass_on(0)
    if columns > 1:
        share_out(1)
    for copy in swaps:
        copy.wait_recv()
    for copy in loads:
        copy.wait()
    for step in range(columns):
        if step >= 1:
            pass_on(step)
            if step + 1 < columns:
                share_out(step + 1)
        if step >= 3:
            reduce_end(step - 3)
        if step >= 2:
            reduce_two(step - 2)
        compute(step)
        reduce_one(step)
    for step in range(max(0, columns - 3), columns + 2):
        if step < columns and step >= columns - 2 and step >= 0:
            reduce_two(step)
        if step - 1 >= max(0, columns - 3) and step - 1 < columns:
            reduce_end(step - 1)
    for step in range(1, columns):
        for copy in ends[step]:
            copy.wait_recv()
    for side in (0, 1):
        def body(index, carry, side=side):
            place = pl.ds(index * 16, 16)
            total = sums[side, 0, place].astype(jnp.float32)
            for step in range(1, columns):
                total = total + finals[side, step - 1, place].astype(jnp.float32)
            totals[place, pl.ds(side * split, split)] = total.astype(jnp.bfloat16)
            return carry

        lax.fori_loop(0, count // 16, body, 0)
    result = pltpu.make_async_copy(totals, out_ref, load_sem.at[0])
    result.start()
    for copy in everything:
        copy.wait_send()
    result.wait()


def by_rows(tokens, expert_ids, gate_weights, w_gate, w_up, w_down):
    nodes, columns = lax.axis_size("node"), lax.axis_size("local") // 2
    experts = nodes * columns
    count, width = tokens.shape
    hidden_half = w_gate.shape[1]
    hits = expert_ids[:, :, None] == jnp.arange(experts, dtype=jnp.int32)[None, None, :]
    table = jnp.sum(jnp.where(hits, gate_weights[:, :, None], 0.0), axis=1)
    pieces = []
    for _ in range(3):
        piece = lax.reduce_precision(table, 8, 7)
        pieces.append(piece.astype(jnp.bfloat16))
        table = table - piece
    pieces = jnp.concatenate(pieces, axis=1)
    pieces = jnp.pad(pieces, ((0, 0), (0, LANES - pieces.shape[1])))
    rows = jnp.concatenate([tokens, pieces], axis=1)
    wide = rows.shape[1]
    split = width // 2
    dma = pltpu.SemaphoreType.DMA
    bf16 = jnp.bfloat16
    scratch = [
        pltpu.VMEM((columns, 4 * count, wide), bf16),
        pltpu.VMEM((width, 4 * hidden_half), bf16),
        pltpu.VMEM((2 * hidden_half, width), bf16),
        pltpu.VMEM((2, columns, 4 * count, split), bf16),
        pltpu.VMEM((2, columns, 2 * count, split), bf16),
        pltpu.VMEM((2, columns, count, split), bf16),
        pltpu.VMEM((2, columns - 1, count, split), bf16),
        pltpu.VMEM((4 * count, 4 * hidden_half), jnp.float32),
        pltpu.VMEM((4 * count, 2 * hidden_half), bf16),
        pltpu.VMEM((count, width), bf16),
        dma((4,)), dma((3,)), dma((3,)), dma((columns,)), dma((columns,)),
    ] + [dma((columns, 2)) for _ in range(10)]
    flops = 12 * experts * count * width * hidden_half
    return pl.pallas_call(
        functools.partial(layer_kernel, nodes, columns, width, hidden_half),
        name="moe_layer",
        out_shape=jax.ShapeDtypeStruct((count, width), bf16),
        in_specs=[pl.BlockSpec(memory_space=pl.ANY)] * 4,
        out_specs=pl.BlockSpec(memory_space=pl.ANY),
        scratch_shapes=scratch,
        cost_estimate=pl.CostEstimate(flops=flops, bytes_accessed=w_gate.size * 12, transcendentals=0),
        compiler_params=pltpu.CompilerParams(collective_id=0, has_side_effects=True, vmem_limit_bytes=60 << 20),
    )(rows, w_gate, w_up, w_down)


def per_device(tokens, expert_ids, *rest):
    nodes, columns = lax.axis_size("node"), lax.axis_size("local") // 2
    dense_enough = nodes * columns <= 2 * expert_ids.shape[1]
    if nodes == 4 and columns & (columns - 1) == 0 and dense_enough:
        return by_rows(tokens, expert_ids, *rest)
    return by_slots(tokens, expert_ids, *rest)


def solution(mesh):
    placed = (
        P(("parts", "node", "local"), None),
        P(("parts", "node", "local"), None),
        P(("parts", "node", "local"), None),
        P(None, ("parts", "node", "local")),
        P(None, ("parts", "node", "local")),
        P(("parts", "node", "local"), None),
    )
    return jax.shard_map(
        per_device,
        mesh=mesh,
        in_specs=placed,
        out_specs=P(("parts", "node", "local"), None),
        check_vma=False,
    )
```

```python
import functools

import jax
import jax.numpy as jnp
from jax import lax
from jax.experimental import pallas as pl
from jax.experimental.pallas import tpu as pltpu
from jax.sharding import PartitionSpec as P

MESH = pl.DeviceIdType.MESH


def partner_2(value, axis, bit):
    mask = 2**bit
    pairs = [(source, source ^ mask) for source in range(lax.axis_size(axis))]
    return lax.ppermute(value, axis, pairs)


def by_slots(tokens, expert_ids, gate_weights, w_gate, w_up, w_down):
    node_count = lax.axis_size("node")
    local_count = lax.axis_size("local")
    devices = node_count * local_count
    experts = devices // 2
    tok_rows, top_count = expert_ids.shape
    width = tokens.shape[1]
    capacity = tok_rows * top_count * 5 // (4 * experts)
    flat_ids = expert_ids.reshape(-1)
    one_hot = (flat_ids[:, None] == jnp.arange(experts, dtype=jnp.int32)[None, :]).astype(jnp.int32)
    earlier = jnp.cumsum(one_hot, axis=0) - one_hot
    slot_rank = jnp.sum(earlier * one_hot, axis=1)
    slot_index = (flat_ids * capacity + slot_rank).reshape(tok_rows, top_count)
    slot_table = jnp.any(
        slot_index[None, :, :] == jnp.arange(experts * capacity, dtype=jnp.int32)[:, None, None],
        axis=2,
    ).astype(jnp.bfloat16)
    outgoing = jnp.dot(slot_table, tokens, preferred_element_type=jnp.float32).astype(jnp.bfloat16)
    outgoing = outgoing.reshape(devices, capacity // 2, width)
    partner = partner_2((w_gate, w_up, w_down), "local", 0)
    full_gate = jnp.concatenate([w_gate, partner[0]], axis=1)
    full_up = jnp.concatenate([w_up, partner[1]], axis=1)
    full_down = jnp.concatenate([w_down, partner[2]], axis=0)
    block = lax.all_to_all(outgoing, ("node", "local"), split_axis=0, concat_axis=0, tiled=True)
    rows = block.reshape(-1, width)
    gate = jnp.dot(rows, full_gate, preferred_element_type=jnp.float32)
    upper = jnp.dot(rows, full_up, preferred_element_type=jnp.float32)
    hidden = (jax.nn.silu(gate) * upper).astype(jnp.bfloat16)
    result = jnp.dot(hidden, full_down, preferred_element_type=jnp.float32).astype(jnp.bfloat16)
    processed = result.reshape(block.shape)
    returned = lax.all_to_all(processed, ("node", "local"), split_axis=0, concat_axis=0, tiled=True)
    results = returned.reshape(experts * capacity, width)
    chosen = results[slot_index]
    mixed = jnp.sum(gate_weights[:, :, None] * chosen.astype(jnp.float32), axis=1)
    return mixed.astype(jnp.bfloat16)


LANES = 128


def layer_kernel(
    nodes, columns, width, hidden_half,
    rows_ref, gate_ref, up_ref, down_ref, out_ref,
    taken, first, second, sums, firsts, seconds, finals, acts, hidden, totals,
    load_sem, swap_send, swap_recv, col_send, col_recv, own_send, own_recv, far_send, far_recv,
    one_send, one_recv, two_send, two_recv, end_send, end_recv,
):
    part, node, local = lax.axis_index("parts"), lax.axis_index("node"), lax.axis_index("local")
    column, half = local // 2, lax.rem(local, 2)
    high, low = node // 2, lax.rem(node, 2)
    count = rows_ref.shape[0]
    split = width // 2
    wide = rows_ref.shape[1]

    def at(node_index, local_index):
        return (part, node_index, local_index)

    sides = (at(high * 2 + 1 - low, local), at((1 - high) * 2 + low, local))
    twin = at(node, column * 2 + 1 - half)

    def along(step):
        low_bit = lax.rem(column, 2)
        if step & 1:
            low_bit = 1 - low_bit
        rest, bit = column // 2, 1
        place = low_bit
        while (1 << bit) < columns:
            value = lax.rem(rest, 2)
            if step >> bit & 1:
                value = 1 - value
            place = place + value * (1 << bit)
            rest, bit = rest // 2, bit + 1
        return at(node, place * 2 + half)

    peers = [along(step) for step in range(1, columns)]
    barrier = pltpu.get_barrier_semaphore()
    for peer in (*sides, twin, *peers):
        pl.semaphore_signal(barrier, inc=1, device_id=peer, device_id_type=MESH)
    pl.semaphore_wait(barrier, 3 + len(peers))

    def send(source, target, send_sem, recv_sem, peer):
        return pltpu.make_async_remote_copy(
            src_ref=source, dst_ref=target, send_sem=send_sem, recv_sem=recv_sem,
            device_id=peer, device_id_type=MESH,
        )

    everything = []

    def start(copy):
        copy.start()
        everything.append(copy)
        return copy

    def block(step, slot):
        return taken.at[step, pl.ds(slot * count, count)]

    def columns_of(side):
        return pl.ds(0, split) if side == 0 else pl.ds(split, wide - split)

    near = (
        (gate_ref, first, 0, False), (up_ref, first, 1, False), (down_ref, second, 0, True),
    )
    loads, swaps = [], []

    def spot(target, index, by_rows, other):
        place = pl.ds((index + other) * hidden_half, hidden_half)
        return target.at[place] if by_rows else target.at[:, place]

    own = [start(send(rows_ref, block(0, side + 1), own_send.at[0, side], own_recv.at[0, side], sides[side])) for side in (0, 1)]
    spread = [start(send(rows_ref, block(step, 0), col_send.at[step], col_recv.at[step], peers[step - 1])) for step in range(1, columns)]
    for number, (source, target, index, by_rows) in enumerate(near):
        swaps.append(start(send(source, spot(target, index, by_rows, 1 if by_rows else 2), swap_send.at[number], swap_recv.at[number], twin)))
    for number, (source, target, index, by_rows) in enumerate(near):
        loads.append(pltpu.make_async_copy(source, spot(target, index, by_rows, 0), load_sem.at[number]))
    loads.append(pltpu.make_async_copy(rows_ref, block(0, 0), load_sem.at[len(near)]))
    for copy in loads:
        copy.start()

    nears, fars = [own], []

    def pass_on(step):
        moved = []
        for side in (0, 1):
            nears[step][side].wait_recv()
            piece = taken.at[step, pl.ds((side + 1) * count, count), columns_of(side)]
            target = taken.at[step, pl.ds(3 * count, count), columns_of(side)]
            moved.append(start(send(piece, target, far_send.at[step, side], far_recv.at[step, side], sides[1 - side])))
        fars.append(moved)

    def share_out(step):
        spread[step - 1].wait_recv()
        nears.append([
            start(send(block(step, 0), block(step, side + 1), own_send.at[step, side], own_recv.at[step, side], sides[side]))
            for side in (0, 1)
        ])

    def compute(step):
        for copy in fars[step]:
            copy.wait_recv()
        expert = node * columns + column
        table = taken[step, :, pl.ds(width, LANES)].astype(jnp.float32)
        lane = lax.broadcasted_iota(jnp.int32, table.shape, 1)
        chosen = (lane == expert) | (lane == expert + nodes * columns) | (lane == expert + 2 * nodes * columns)
        share = jnp.sum(jnp.where(chosen, table, 0.0), axis=1, keepdims=True)
        tile = 2 * LANES

        def into(index, carry):
            place = pl.ds(pl.multiple_of(index * tile, tile), tile)
            acts[:, place] = jnp.dot(taken[step, :, pl.ds(0, width)], first[:, place], preferred_element_type=jnp.float32)
            return carry

        lax.fori_loop(0, acts.shape[1] // tile, into, 0)
        for other in (0, 1):
            gate = acts[:, pl.ds(2 * other * hidden_half, hidden_half)]
            upper = acts[:, pl.ds((2 * other + 1) * hidden_half, hidden_half)]
            hidden[:, pl.ds(other * hidden_half, hidden_half)] = (gate / (1.0 + jnp.exp(-gate)) * upper).astype(jnp.bfloat16)
        share_wide = jnp.broadcast_to(share, (4 * count, tile))
        for side in (0, 1):
            def out_of(index, carry, side=side):
                place = pl.ds(pl.multiple_of(index * tile, tile), tile)
                source = pl.ds(pl.multiple_of(side * split + index * tile, tile), tile)
                result = jnp.dot(hidden[...], second[:, source], preferred_element_type=jnp.float32)
                result = (result * share_wide).astype(jnp.bfloat16)
                order = (0, 2, 1, 3) if side == 0 else (0, 1, 2, 3)
                for slot in range(4):
                    sums[side, step, pl.ds(order[slot] * count, count), place] = result[slot * count:(slot + 1) * count]
                return carry

            lax.fori_loop(0, split // tile, out_of, 0)

    ones, twos, ends = {}, {}, {}

    def reduce_one(step):
        ones[step] = [
            start(send(sums.at[side, step, pl.ds(2 * count, 2 * count)], firsts.at[side, step], one_send.at[step, side], one_recv.at[step, side], sides[side]))
            for side in (0, 1)
        ]

    def add(side, step, start_row, rows, source):
        def body(index, carry):
            place = pl.ds(start_row + index * 16, 16)
            other = pl.ds(index * 16, 16)
            total = sums[side, step, place].astype(jnp.float32) + source[side, step, other].astype(jnp.float32)
            sums[side, step, place] = total.astype(jnp.bfloat16)
            return carry

        lax.fori_loop(0, rows // 16, body, 0)

    def reduce_two(step):
        twos[step] = []
        for side in (0, 1):
            ones[step][side].wait_recv()
            add(side, step, 0, 2 * count, firsts)
            twos[step].append(start(send(sums.at[side, step, pl.ds(count, count)], seconds.at[side, step], two_send.at[step, side], two_recv.at[step, side], sides[1 - side])))

    def reduce_end(step):
        for side in (0, 1):
            twos[step][side].wait_recv()
            add(side, step, 0, count, seconds)
        if step:
            ends[step] = [
                start(send(sums.at[side, step, pl.ds(0, count)], finals.at[side, step - 1], end_send.at[step, side], end_recv.at[step, side], peers[step - 1]))
                for side in (0, 1)
            ]

    last = columns - 1
    pass_on(0)
    if last:
        share_out(1)
    for copy in swaps:
        copy.wait_recv()
    for copy in loads:
        copy.wait()
    if last:
        pass_on(1)
    compute(0)
    for step in range(1, columns):
        if step >= 2 and step < last:
            share_out(step + 1)
            reduce_two(step - 1)
        elif step == 1 and step < last:
            share_out(2)
        compute(step)
        if step == 1 and step < last:
            reduce_one(1)
            pass_on(2)
            continue
        if step < last:
            pass_on(step + 1)
        reduce_one(step)
        if step < last:
            reduce_end(step - 1)
    if last >= 2:
        reduce_two(last - 1)
    if last:
        reduce_two(last)
    reduce_one(0)
    if last >= 2:
        reduce_end(last - 1)
    if last:
        reduce_end(last)
    reduce_two(0)
    reduce_end(0)
    for step in range(1, columns):
        for copy in ends[step]:
            copy.wait_recv()
    for side in (0, 1):
        def body(index, carry, side=side):
            place = pl.ds(index * 16, 16)
            total = sums[side, 0, place].astype(jnp.float32)
            for step in range(1, columns):
                total = total + finals[side, step - 1, place].astype(jnp.float32)
            totals[place, pl.ds(side * split, split)] = total.astype(jnp.bfloat16)
            return carry

        lax.fori_loop(0, count // 16, body, 0)
    result = pltpu.make_async_copy(totals, out_ref, load_sem.at[0])
    result.start()
    for copy in everything:
        copy.wait_send()
    result.wait()


def by_rows(tokens, expert_ids, gate_weights, w_gate, w_up, w_down):
    nodes, columns = lax.axis_size("node"), lax.axis_size("local") // 2
    experts = nodes * columns
    count, width = tokens.shape
    hidden_half = w_gate.shape[1]
    hits = expert_ids[:, :, None] == jnp.arange(experts, dtype=jnp.int32)[None, None, :]
    table = jnp.sum(jnp.where(hits, gate_weights[:, :, None], 0.0), axis=1)
    pieces = []
    for _ in range(3):
        piece = lax.reduce_precision(table, 8, 7)
        pieces.append(piece.astype(jnp.bfloat16))
        table = table - piece
    pieces = jnp.concatenate(pieces, axis=1)
    pieces = jnp.pad(pieces, ((0, 0), (0, LANES - pieces.shape[1])))
    rows = jnp.concatenate([tokens, pieces], axis=1)
    wide = rows.shape[1]
    split = width // 2
    dma = pltpu.SemaphoreType.DMA
    bf16 = jnp.bfloat16
    scratch = [
        pltpu.VMEM((columns, 4 * count, wide), bf16),
        pltpu.VMEM((width, 4 * hidden_half), bf16),
        pltpu.VMEM((2 * hidden_half, width), bf16),
        pltpu.VMEM((2, columns, 4 * count, split), bf16),
        pltpu.VMEM((2, columns, 2 * count, split), bf16),
        pltpu.VMEM((2, columns, count, split), bf16),
        pltpu.VMEM((2, columns - 1, count, split), bf16),
        pltpu.VMEM((4 * count, 4 * hidden_half), jnp.float32),
        pltpu.VMEM((4 * count, 2 * hidden_half), bf16),
        pltpu.VMEM((count, width), bf16),
        dma((4,)), dma((3,)), dma((3,)), dma((columns,)), dma((columns,)),
    ] + [dma((columns, 2)) for _ in range(10)]
    flops = 12 * experts * count * width * hidden_half
    return pl.pallas_call(
        functools.partial(layer_kernel, nodes, columns, width, hidden_half),
        name="moe_layer",
        out_shape=jax.ShapeDtypeStruct((count, width), bf16),
        in_specs=[pl.BlockSpec(memory_space=pl.ANY)] * 4,
        out_specs=pl.BlockSpec(memory_space=pl.ANY),
        scratch_shapes=scratch,
        cost_estimate=pl.CostEstimate(flops=flops, bytes_accessed=w_gate.size * 12, transcendentals=0),
        compiler_params=pltpu.CompilerParams(collective_id=0, has_side_effects=True, vmem_limit_bytes=60 << 20),
    )(rows, w_gate, w_up, w_down)


def per_device(tokens, expert_ids, *rest):
    nodes, columns = lax.axis_size("node"), lax.axis_size("local") // 2
    dense_enough = nodes * columns <= 2 * expert_ids.shape[1]
    if nodes == 4 and columns & (columns - 1) == 0 and dense_enough:
        return by_rows(tokens, expert_ids, *rest)
    return by_slots(tokens, expert_ids, *rest)


def solution(mesh):
    placed = (
        P(("parts", "node", "local"), None),
        P(("parts", "node", "local"), None),
        P(("parts", "node", "local"), None),
        P(None, ("parts", "node", "local")),
        P(None, ("parts", "node", "local")),
        P(("parts", "node", "local"), None),
    )
    return jax.shard_map(
        per_device,
        mesh=mesh,
        in_specs=placed,
        out_specs=P(("parts", "node", "local"), None),
        check_vma=False,
    )
```

```python
import functools

import jax
import jax.numpy as jnp
from jax import lax
from jax.experimental import pallas as pl
from jax.experimental.pallas import tpu as pltpu
from jax.sharding import PartitionSpec as P

MESH = pl.DeviceIdType.MESH


def partner_2(value, axis, bit):
    mask = 2**bit
    pairs = [(source, source ^ mask) for source in range(lax.axis_size(axis))]
    return lax.ppermute(value, axis, pairs)


def by_slots(tokens, expert_ids, gate_weights, w_gate, w_up, w_down):
    node_count = lax.axis_size("node")
    local_count = lax.axis_size("local")
    devices = node_count * local_count
    experts = devices // 2
    tok_rows, top_count = expert_ids.shape
    width = tokens.shape[1]
    capacity = tok_rows * top_count * 5 // (4 * experts)
    flat_ids = expert_ids.reshape(-1)
    one_hot = (flat_ids[:, None] == jnp.arange(experts, dtype=jnp.int32)[None, :]).astype(jnp.int32)
    earlier = jnp.cumsum(one_hot, axis=0) - one_hot
    slot_rank = jnp.sum(earlier * one_hot, axis=1)
    slot_index = (flat_ids * capacity + slot_rank).reshape(tok_rows, top_count)
    slot_table = jnp.any(
        slot_index[None, :, :] == jnp.arange(experts * capacity, dtype=jnp.int32)[:, None, None],
        axis=2,
    ).astype(jnp.bfloat16)
    outgoing = jnp.dot(slot_table, tokens, preferred_element_type=jnp.float32).astype(jnp.bfloat16)
    outgoing = outgoing.reshape(devices, capacity // 2, width)
    partner = partner_2((w_gate, w_up, w_down), "local", 0)
    full_gate = jnp.concatenate([w_gate, partner[0]], axis=1)
    full_up = jnp.concatenate([w_up, partner[1]], axis=1)
    full_down = jnp.concatenate([w_down, partner[2]], axis=0)
    block = lax.all_to_all(outgoing, ("node", "local"), split_axis=0, concat_axis=0, tiled=True)
    rows = block.reshape(-1, width)
    gate = jnp.dot(rows, full_gate, preferred_element_type=jnp.float32)
    upper = jnp.dot(rows, full_up, preferred_element_type=jnp.float32)
    hidden = (jax.nn.silu(gate) * upper).astype(jnp.bfloat16)
    result = jnp.dot(hidden, full_down, preferred_element_type=jnp.float32).astype(jnp.bfloat16)
    processed = result.reshape(block.shape)
    returned = lax.all_to_all(processed, ("node", "local"), split_axis=0, concat_axis=0, tiled=True)
    results = returned.reshape(experts * capacity, width)
    chosen = results[slot_index]
    mixed = jnp.sum(gate_weights[:, :, None] * chosen.astype(jnp.float32), axis=1)
    return mixed.astype(jnp.bfloat16)


LANES = 128


def layer_kernel(
    nodes, columns, width, hidden_half, extra,
    rows_ref, gate_ref, up_ref, down_ref, out_ref,
    taken, first, second, sums, firsts, seconds, finals, acts, hidden, totals,
    load_sem, swap_send, swap_recv, col_send, col_recv, own_send, own_recv, far_send, far_recv,
    one_send, one_recv, two_send, two_recv, end_send, end_recv,
    early_send, early_recv, late_send, late_recv, lates,
):
    part, node, local = lax.axis_index("parts"), lax.axis_index("node"), lax.axis_index("local")
    column, half = local // 2, lax.rem(local, 2)
    high, low = node // 2, lax.rem(node, 2)
    count = rows_ref.shape[0]
    split = width // 2
    wide = rows_ref.shape[1]
    middle = LANES + (width - extra) // 2
    body_end = wide - extra
    kept = split - extra // 2

    def at(node_index, local_index):
        return (part, node_index, local_index)

    sides = (at(high * 2 + 1 - low, local), at((1 - high) * 2 + low, local))
    twin = at(node, column * 2 + 1 - half)

    def along(step):
        low_bit = lax.rem(column, 2)
        if step & 1:
            low_bit = 1 - low_bit
        rest, bit = column // 2, 1
        place = low_bit
        while (1 << bit) < columns:
            value = lax.rem(rest, 2)
            if step >> bit & 1:
                value = 1 - value
            place = place + value * (1 << bit)
            rest, bit = rest // 2, bit + 1
        return at(node, place * 2 + half)

    peers = [along(step) for step in range(1, columns)]
    barrier = pltpu.get_barrier_semaphore()
    for peer in (*sides, twin, *peers):
        pl.semaphore_signal(barrier, inc=1, device_id=peer, device_id_type=MESH)
    pl.semaphore_wait(barrier, 3 + len(peers))

    def send(source, target, send_sem, recv_sem, peer):
        return pltpu.make_async_remote_copy(
            src_ref=source, dst_ref=target, send_sem=send_sem, recv_sem=recv_sem,
            device_id=peer, device_id_type=MESH,
        )

    everything = []

    def start(copy):
        copy.start()
        everything.append(copy)
        return copy

    def block(step, slot):
        return taken.at[step, pl.ds(slot * count, count)]

    def columns_of(step, side):
        end = body_end if step else wide
        return pl.ds(0, middle) if side == 0 else pl.ds(middle, end - middle)

    near = (
        (gate_ref, first, 0, False), (up_ref, first, 1, False), (down_ref, second, 0, True),
    )
    loads, swaps = [], []

    def spot(target, index, by_rows, other):
        place = pl.ds((index + other) * hidden_half, hidden_half)
        return target.at[place] if by_rows else target.at[:, place]

    own = [start(send(rows_ref, block(0, side + 1), own_send.at[0, side], own_recv.at[0, side], sides[side])) for side in (0, 1)]
    spread = [start(send(rows_ref.at[:, pl.ds(0, body_end)], block(step, 0).at[:, pl.ds(0, body_end)], col_send.at[step], col_recv.at[step], peers[step - 1])) for step in range(1, columns)]
    for number, (source, target, index, by_rows) in enumerate(near):
        swaps.append(start(send(source, spot(target, index, by_rows, 1 if by_rows else 2), swap_send.at[number], swap_recv.at[number], twin)))
    for number, (source, target, index, by_rows) in enumerate(near):
        loads.append(pltpu.make_async_copy(source, spot(target, index, by_rows, 0), load_sem.at[number]))
    loads.append(pltpu.make_async_copy(rows_ref, block(0, 0), load_sem.at[len(near)]))
    for copy in loads:
        copy.start()

    nears, fars = [own], []

    def pass_on(step):
        moved = []
        for side in (0, 1):
            nears[step][side].wait_recv()
            piece = taken.at[step, pl.ds((side + 1) * count, count), columns_of(step, side)]
            target = taken.at[step, pl.ds(3 * count, count), columns_of(step, side)]
            moved.append(start(send(piece, target, far_send.at[step, side], far_recv.at[step, side], sides[1 - side])))
        fars.append(moved)

    def share_out(step):
        spread[step - 1].wait_recv()
        nears.append([
            start(send(block(step, 0).at[:, pl.ds(0, body_end)], block(step, side + 1).at[:, pl.ds(0, body_end)], own_send.at[step, side], own_recv.at[step, side], sides[side]))
            for side in (0, 1)
        ])

    earlies, late = {}, {}

    def spread_extra():
        for copy in fars[0]:
            copy.wait_recv()
        place = pl.ds(body_end, extra)
        for step in range(1, columns):
            earlies[step] = start(send(taken.at[0, :, place], taken.at[step, :, place], early_send.at[step], early_recv.at[step], peers[step - 1]))

    def compute(step):
        if step:
            for copy in fars[step]:
                copy.wait_recv()
            earlies[step].wait_recv()
        expert = node * columns + column
        table = taken[step, :, pl.ds(0, LANES)].astype(jnp.float32)
        lane = lax.broadcasted_iota(jnp.int32, table.shape, 1)
        chosen = (lane == expert) | (lane == expert + nodes * columns) | (lane == expert + 2 * nodes * columns)
        share = jnp.sum(jnp.where(chosen, table, 0.0), axis=1, keepdims=True)
        tile = 2 * LANES

        def into(index, carry):
            place = pl.ds(pl.multiple_of(index * tile, tile), tile)
            acts[:, place] = jnp.dot(taken[step, :, pl.ds(LANES, width)], first[:, place], preferred_element_type=jnp.float32)
            return carry

        lax.fori_loop(0, acts.shape[1] // tile, into, 0)
        for other in (0, 1):
            gate = acts[:, pl.ds(2 * other * hidden_half, hidden_half)]
            upper = acts[:, pl.ds((2 * other + 1) * hidden_half, hidden_half)]
            hidden[:, pl.ds(other * hidden_half, hidden_half)] = (gate / (1.0 + jnp.exp(-gate)) * upper).astype(jnp.bfloat16)
        share_wide = jnp.broadcast_to(share, (4 * count, tile))
        for side in (0, 1):
            def out_of(index, carry, side=side):
                place = pl.ds(pl.multiple_of(index * tile, tile), tile)
                source = pl.ds(pl.multiple_of(side * split + index * tile, tile), tile)
                result = jnp.dot(hidden[...], second[:, source], preferred_element_type=jnp.float32)
                result = (result * share_wide).astype(jnp.bfloat16)
                order = (0, 2, 1, 3) if side == 0 else (0, 1, 2, 3)
                for slot in range(4):
                    sums[side, step, pl.ds(order[slot] * count, count), place] = result[slot * count:(slot + 1) * count]
                return carry

            lax.fori_loop(0, split // tile, out_of, 0)
        if step:
            place = pl.ds(kept, split - kept)
            late[step] = [
                start(send(sums.at[side, step, :, place], lates.at[side, step - 1], late_send.at[step, side], late_recv.at[step, side], peers[step - 1]))
                for side in (0, 1)
            ]

    def span(step):
        return pl.ds(0, kept if step else split)

    def gather_late():
        for step in range(1, columns):
            for copy in late[step]:
                copy.wait_recv()
        place = pl.ds(kept, split - kept)
        for side in (0, 1):
            def body(index, carry, side=side):
                rows = pl.ds(index * 16, 16)
                total = sums[side, 0, rows, place].astype(jnp.float32)
                for step in range(1, columns):
                    total = total + lates[side, step - 1, rows].astype(jnp.float32)
                sums[side, 0, rows, place] = total.astype(jnp.bfloat16)
                return carry

            lax.fori_loop(0, 4 * count // 16, body, 0)

    ones, twos, ends = {}, {}, {}

    def reduce_one(step):
        ones[step] = [
            start(send(sums.at[side, step, pl.ds(2 * count, 2 * count), span(step)], firsts.at[side, step, :, span(step)], one_send.at[step, side], one_recv.at[step, side], sides[side]))
            for side in (0, 1)
        ]

    def add(side, step, start_row, rows, source):
        def body(index, carry):
            place = pl.ds(start_row + index * 16, 16)
            other = pl.ds(index * 16, 16)
            lanes = span(step)
            total = sums[side, step, place, lanes].astype(jnp.float32) + source[side, step, other, lanes].astype(jnp.float32)
            sums[side, step, place, lanes] = total.astype(jnp.bfloat16)
            return carry

        lax.fori_loop(0, rows // 16, body, 0)

    def reduce_two(step):
        twos[step] = []
        for side in (0, 1):
            ones[step][side].wait_recv()
            add(side, step, 0, 2 * count, firsts)
            twos[step].append(start(send(sums.at[side, step, pl.ds(count, count), span(step)], seconds.at[side, step, :, span(step)], two_send.at[step, side], two_recv.at[step, side], sides[1 - side])))

    def reduce_end(step):
        for side in (0, 1):
            twos[step][side].wait_recv()
            add(side, step, 0, count, seconds)
        if step:
            ends[step] = [
                start(send(sums.at[side, step, pl.ds(0, count), span(step)], finals.at[side, step - 1], end_send.at[step, side], end_recv.at[step, side], peers[step - 1]))
                for side in (0, 1)
            ]

    last = columns - 1
    pass_on(0)
    if last:
        share_out(1)
    for copy in swaps:
        copy.wait_recv()
    for copy in loads:
        copy.wait()
    spread_extra()
    if last:
        pass_on(1)
    compute(0)
    for step in range(1, columns):
        if step >= 2 and step < last:
            share_out(step + 1)
            reduce_two(step - 1)
        elif step == 1 and step < last:
            share_out(2)
        compute(step)
        if step == 1 and step < last:
            reduce_one(1)
            pass_on(2)
            continue
        if step < last:
            pass_on(step + 1)
        reduce_one(step)
        if step < last:
            reduce_end(step - 1)
    if last >= 2:
        reduce_two(last - 1)
    if last:
        reduce_two(last)
    gather_late()
    reduce_one(0)
    if last >= 2:
        reduce_end(last - 1)
    if last:
        reduce_end(last)
    reduce_two(0)
    reduce_end(0)
    for step in range(1, columns):
        for copy in ends[step]:
            copy.wait_recv()
    for side in (0, 1):
        def body(index, carry, side=side):
            place = pl.ds(index * 16, 16)
            total = sums[side, 0, place, pl.ds(0, kept)].astype(jnp.float32)
            for step in range(1, columns):
                total = total + finals[side, step - 1, place].astype(jnp.float32)
            totals[place, pl.ds(side * split, kept)] = total.astype(jnp.bfloat16)
            totals[place, pl.ds(side * split + kept, split - kept)] = sums[side, 0, place, pl.ds(kept, split - kept)]
            return carry

        lax.fori_loop(0, count // 16, body, 0)
    result = pltpu.make_async_copy(totals, out_ref, load_sem.at[0])
    result.start()
    for copy in everything:
        copy.wait_send()
    result.wait()


def by_rows(tokens, expert_ids, gate_weights, w_gate, w_up, w_down):
    nodes, columns = lax.axis_size("node"), lax.axis_size("local") // 2
    experts = nodes * columns
    count, width = tokens.shape
    hidden_half = w_gate.shape[1]
    hits = expert_ids[:, :, None] == jnp.arange(experts, dtype=jnp.int32)[None, None, :]
    table = jnp.sum(jnp.where(hits, gate_weights[:, :, None], 0.0), axis=1)
    pieces = []
    for _ in range(3):
        piece = lax.reduce_precision(table, 8, 7)
        pieces.append(piece.astype(jnp.bfloat16))
        table = table - piece
    pieces = jnp.concatenate(pieces, axis=1)
    pieces = jnp.pad(pieces, ((0, 0), (0, LANES - pieces.shape[1])))
    rows = jnp.concatenate([pieces, tokens], axis=1)
    wide = rows.shape[1]
    split = width // 2
    extra = width // 8
    kept = split - extra // 2
    dma = pltpu.SemaphoreType.DMA
    bf16 = jnp.bfloat16
    scratch = [
        pltpu.VMEM((columns, 4 * count, wide), bf16),
        pltpu.VMEM((width, 4 * hidden_half), bf16),
        pltpu.VMEM((2 * hidden_half, width), bf16),
        pltpu.VMEM((2, columns, 4 * count, split), bf16),
        pltpu.VMEM((2, columns, 2 * count, split), bf16),
        pltpu.VMEM((2, columns, count, split), bf16),
        pltpu.VMEM((2, columns - 1, count, kept), bf16),
        pltpu.VMEM((4 * count, 4 * hidden_half), jnp.float32),
        pltpu.VMEM((4 * count, 2 * hidden_half), bf16),
        pltpu.VMEM((count, width), bf16),
        dma((4,)), dma((3,)), dma((3,)), dma((columns,)), dma((columns,)),
    ] + [dma((columns, 2)) for _ in range(10)] + [
        dma((columns,)), dma((columns,)), dma((columns, 2)), dma((columns, 2)),
        pltpu.VMEM((2, columns - 1, 4 * count, split - kept), bf16),
    ]
    flops = 12 * experts * count * width * hidden_half
    return pl.pallas_call(
        functools.partial(layer_kernel, nodes, columns, width, hidden_half, extra),
        name="moe_layer",
        out_shape=jax.ShapeDtypeStruct((count, width), bf16),
        in_specs=[pl.BlockSpec(memory_space=pl.ANY)] * 4,
        out_specs=pl.BlockSpec(memory_space=pl.ANY),
        scratch_shapes=scratch,
        cost_estimate=pl.CostEstimate(flops=flops, bytes_accessed=w_gate.size * 12, transcendentals=0),
        compiler_params=pltpu.CompilerParams(collective_id=0, has_side_effects=True, vmem_limit_bytes=60 << 20),
    )(rows, w_gate, w_up, w_down)


def per_device(tokens, expert_ids, *rest):
    nodes, columns = lax.axis_size("node"), lax.axis_size("local") // 2
    dense_enough = nodes * columns <= 2 * expert_ids.shape[1]
    if nodes == 4 and columns & (columns - 1) == 0 and dense_enough:
        return by_rows(tokens, expert_ids, *rest)
    return by_slots(tokens, expert_ids, *rest)


def solution(mesh):
    placed = (
        P(("parts", "node", "local"), None),
        P(("parts", "node", "local"), None),
        P(("parts", "node", "local"), None),
        P(None, ("parts", "node", "local")),
        P(None, ("parts", "node", "local")),
        P(("parts", "node", "local"), None),
    )
    return jax.shard_map(
        per_device,
        mesh=mesh,
        in_specs=placed,
        out_specs=P(("parts", "node", "local"), None),
        check_vma=False,
    )
```
